256 devices in a mesh: rep: 16 (over z, core), rows: 16 (over y, x).
Axes of the slice: x: 4, y: 4, z: 8, core: 2. Of those that a mesh axis runs over, the one named last changes fastest.
Arguments:
- weights: bfloat16 [7168, 2048], P('rows'), may hold values from -6 to 6
- momentum: float32 [16, 7168, 2048], P('rep', 'rows'), may hold values from -8 to 8
- gradient: bfloat16 [16, 7168, 2048], P('rep', 'rows'), may hold values from -8 to 8
- right_factor: float32 [2048, 512], P('rows'), may hold values from -6 to 6
Outputs:
- new_weights: bfloat16 [7168, 2048], P('rows')
- new_momentum: float32 [16, 7168, 2048], P('rep', 'rows')
- new_right: float32 [2048, 512], P('rows')
The draws below stay inside these ranges and needn't reach their ends.
All inputs are finite; a program needn't handle non-finite values.
Results may differ from the reference program's by a relative error of at most 0.019.
Values may be sent and summed in bfloat16 or wider, within the bound.
No kernel may reach another device: no remote copies, remote signals or barrier semaphores. Data moves between devices by JAX's collectives and lax.ppermute only.
A program may use at most 64 MiB of HBM per device.

```python
import math
import jax
import jax.numpy as jnp
from jax import lax

M = 7168
N = 2048
RANK = 512
GROUPS = 16


def shared_signal(key):
    rank_part = RANK // 2
    left_part = jax.random.normal(jax.random.fold_in(key, 101), (M, rank_part), jnp.float32)
    right_part = jax.random.normal(jax.random.fold_in(key, 202), (rank_part, N), jnp.float32)
    signal = jnp.dot(left_part, right_part, precision=lax.Precision.HIGHEST) / math.sqrt(rank_part)
    return signal


def noise_of(key, offset_key):
    sub_key = jax.random.fold_in(key, offset_key)
    return 0.5 * jax.random.normal(sub_key, (GROUPS, M, N), jnp.float32)


def draw_momentum(key, part):
    signal = shared_signal(key)
    values = 0.6 * signal[None] + noise_of(key, 11)
    return jnp.clip(values, -8.0, 8.0).astype(jnp.float32)


def draw_gradient(key, part):
    signal = shared_signal(key)
    values = 0.2 * signal[None] + noise_of(key, 12)
    return jnp.clip(values, -8.0, 8.0).astype(jnp.bfloat16)


def steps_of(key, extent, shards, least, largest):
    gain, own = 1.0, jax.random.fold_in(key, 6)
    for axis_at, shards_of in shards:
        steps = jnp.exp(jax.random.uniform(jax.random.fold_in(own, axis_at), (shards_of,), jnp.float32, least / len(shards), largest / len(shards)))
        gain = gain * jnp.repeat(steps, extent[axis_at] // shards_of).reshape([-1 if axis == axis_at else 1 for axis in range(len(extent))])
    return gain


def gaussian(key, extent, spread, most, shards=(), kind=jnp.bfloat16):
    array = jax.random.normal(key, extent, jnp.float32) * spread
    if len(shards) > 0:
        array = steps_of(key, extent, shards, -0.22, 0.18) * array
    return jnp.clip(array, min=-most, max=most).astype(kind)


def setup_inputs(seed: int = 0) -> dict:
    seeds = jax.random.split(jax.random.key(seed), 5)
    weights = gaussian(seeds[0], (M, N), 1.0, 6.0, ((0, 16),))
    momentum = draw_momentum(jax.random.fold_in(seeds[4], 71), 0)
    gradient = draw_gradient(jax.random.fold_in(seeds[4], 71), 0)
    right_factor = gaussian(seeds[3], (N, RANK), 1.0, 6.0, ((0, 16),), jnp.float32)
    return dict(weights=weights, momentum=momentum, gradient=gradient, right_factor=right_factor)


momentum_keep = 0.05
learn_rate = 0.5
tiny = 1e-06

def reference(weights, momentum, gradient, right_factor):
    right_half = right_factor.astype(jnp.bfloat16)

    def left_of(pair):
        mom, grad = pair
        combined_half = (mom + grad.astype(jnp.float32)).astype(jnp.bfloat16)
        left = jnp.dot(combined_half.astype(jnp.float32), right_half.astype(jnp.float32), preferred_element_type=jnp.float32).astype(jnp.bfloat16)
        return lax.optimization_barrier(left).astype(jnp.float32)
    left_each = lax.map(left_of, (momentum, gradient))
    left_mean = lax.optimization_barrier(jnp.sum(left_each, 0)) / GROUPS
    gram = jnp.dot(left_mean.T, left_mean, precision=lax.Precision.HIGHEST)
    chol = jnp.linalg.cholesky(gram)
    left_orth = jax.scipy.linalg.solve_triangular(chol, left_mean.T, lower=True).T
    left_half = left_orth.astype(jnp.bfloat16)

    def right_of(pair):
        mom, grad = pair
        combined_half = (mom + grad.astype(jnp.float32)).astype(jnp.bfloat16)
        return jnp.dot(combined_half.T.astype(jnp.float32), left_half.astype(jnp.float32), preferred_element_type=jnp.float32)
    right_mean = lax.optimization_barrier(jnp.sum(lax.map(right_of, (momentum, gradient)), 0)) / GROUPS
    feedback = jnp.dot(left_half.astype(jnp.float32), right_mean.astype(jnp.bfloat16).T.astype(jnp.float32), preferred_element_type=jnp.float32)

    def moment_of(pair):
        mom, grad = pair
        return mom + grad.astype(jnp.float32) - momentum_keep * feedback
    new_momentum = lax.map(moment_of, (momentum, gradient))
    new_right = right_mean / jnp.sqrt(lax.optimization_barrier(jnp.mean(right_mean * right_mean, axis=0)) + tiny)
    update = jnp.dot(left_half.astype(jnp.float32), new_right.astype(jnp.bfloat16).T.astype(jnp.float32), preferred_element_type=jnp.float32)
    new_weights = (weights.astype(jnp.float32) - learn_rate * jnp.sqrt(M / N) * update).astype(jnp.bfloat16)
    return (new_weights, new_momentum, new_right)
```

```python
import jax
import jax.numpy as jnp
from jax import lax
from jax.experimental import pallas as pl
from jax.experimental.pallas import tpu as pltpu
from jax.sharding import Mesh
from jax.sharding import PartitionSpec as P

M = 7168
N = 2048
ROWS = ("y", "x")
REP = ("z", "c")
SWAP = [(0, 1), (1, 0)]
PANEL = 128
HI = lax.Precision.HIGHEST
f32 = jnp.float32
bf16 = jnp.bfloat16

momentum_keep = 0.05
learn_rate = 0.5
tiny = 1e-06


def eliminate(block):
    sub = lax.broadcasted_iota(jnp.int32, (8, PANEL), 0)
    lane = lax.broadcasted_iota(jnp.int32, (8, PANEL), 1)
    tiles = PANEL // 8
    rows = [block[8 * r : 8 * r + 8, :] for r in range(tiles)]
    pivots = []
    for m in range(tiles):
        here = (lane >= 8 * m) & (lane < 8 * m + 8)
        at = [8 * m + k for k in range(8)]
        cols = [jnp.broadcast_to(rows[m][:, i : i + 1], (8, PANEL)) for i in at]
        low = jnp.where(here, jnp.where(lane - 8 * m == sub, 1.0, 0.0), rows[m])
        full = low
        pivot = jnp.zeros((8, PANEL), f32)
        for k in range(8):
            col = cols[k]
            head = jnp.broadcast_to(col[k : k + 1, :], (8, PANEL))
            inv = 1.0 / head
            pivot = jnp.where(sub == k, head, pivot)

            def step(value):
                row = jnp.broadcast_to(value[k : k + 1, :], (8, PANEL)) * inv
                return jnp.where(sub == k, row, value - col * row)

            if k < 7:
                row = jnp.broadcast_to(low[k : k + 1, :], (8, PANEL)) * inv
                low = jnp.where(sub > k, low - col * row, low)
            cols = [step(other) if n > k else other for n, other in enumerate(cols)]
            full = step(full)
        solved = [jnp.broadcast_to(full[k : k + 1, :], (8, PANEL)) for k in range(8)]
        for r in range(m + 1, tiles):
            parts = [
                jnp.broadcast_to(rows[r][:, i : i + 1], (8, PANEL)) * solved[k]
                for k, i in enumerate(at)
            ]
            while len(parts) > 1:
                parts = [parts[n] + parts[n + 1] for n in range(0, len(parts), 2)]
            rows[r] = jnp.where(here, 0.0, rows[r]) - parts[0]
        rows[m] = low
        pivots.append(pivot)
    return jnp.concatenate(rows, 0), jnp.concatenate(pivots, 0)


def exact_dot(a, b, dim=1):
    return lax.dot_general(a, b, (((dim,), (0,)), ((), ())), precision=HI, preferred_element_type=f32)


def inverse_kernel(first_ref, second_ref, out_ref, work_ref):
    size = out_ref.shape[0]
    half = size // 2
    work_ref[:half, :half] = first_ref[:, :half]
    work_ref[:half, half : half + PANEL] = first_ref[:, half:]
    work_ref[:half, half + PANEL :] = second_ref[:, half:]
    work_ref[half:, half:] = second_ref[:, :half]
    row = lax.broadcasted_iota(jnp.int32, (PANEL, PANEL), 0)
    lane = lax.broadcasted_iota(jnp.int32, (PANEL, PANEL), 1)
    for p in range(size // PANEL):
        a, b = p * PANEL, (p + 1) * PANEL
        packed, pivot = eliminate(work_ref[a:b, a:b])
        lower = jnp.where(lane <= row, packed, 0.0)
        scale = lax.rsqrt(pivot)
        out_ref[a:b, a:b] = lower * scale
        if p > 0:
            left = exact_dot(lower, work_ref[a:b, :a])
            out_ref[a:b, :a] = left * jnp.concatenate([scale] * p, 1)
        if b < size:
            out_ref[a:b, b:] = jnp.zeros((PANEL, size - b), f32)
            right = exact_dot(lower, work_ref[a:b, b:])
            down = right * jnp.concatenate([1.0 / pivot] * ((size - b) // PANEL), 1)
            work_ref[b:, b:] = work_ref[b:, b:] - exact_dot(down, right, 0)
            work_ref[b:, a:b] = -exact_dot(down, lower, 0)
            if p > 0:
                work_ref[b:, :a] = work_ref[b:, :a] - exact_dot(down, left, 0)


def inverse_factor(first, second):
    size = 2 * first.shape[0]
    space = pl.BlockSpec(memory_space=pltpu.VMEM)
    return pl.pallas_call(
        inverse_kernel,
        out_shape=jax.ShapeDtypeStruct((size, size), f32),
        in_specs=[space, space],
        out_specs=space,
        scratch_shapes=[pltpu.VMEM((size, size), f32)],
        cost_estimate=pl.CostEstimate(
            flops=12_000_000_000, bytes_accessed=2_000_000, transcendentals=1000
        ),
        name="inverse_factor",
    )(first, second)


def exchange(value, axes):
    return lax.all_to_all(value, axes, 0, 0, tiled=True)


def gather(value, axes):
    size = lax.axis_size(axes)
    return exchange(jnp.broadcast_to(value[None], (size, *value.shape)), axes)


def partner(value):
    return lax.ppermute(value, "c", SWAP)


def in_order(mine, theirs, core):
    first = jnp.where(core == 0, mine, theirs)
    second = jnp.where(core == 0, theirs, mine)
    return first, second


def per_device(weights, momentum, gradient, right_factor):
    core = lax.axis_index("c")
    depth = lax.axis_size("z")
    blocks = lax.axis_size(ROWS)
    groups = depth * lax.axis_size("c")
    me = lax.axis_index(ROWS)
    rank = right_factor.shape[1]
    half = rank // 2
    rows, columns = momentum.shape[1:]

    right_half = lax.dynamic_slice_in_dim(right_factor, core * half, half, 1).astype(bf16)
    right_half = gather(right_half, ROWS).reshape(columns, half)

    combined = momentum[0] + gradient[0].astype(f32)
    mine = combined.astype(bf16)
    theirs = partner(mine)

    left = jnp.dot(mine, right_half, preferred_element_type=f32) + jnp.dot(
        theirs, right_half, preferred_element_type=f32
    )
    left = exchange(left.astype(bf16).reshape(depth, rows // depth, half), "z")
    left = left.astype(f32).sum(0) / groups
    left = gather(left, "z").reshape(rows, half)
    first, second = in_order(left, partner(left), core)
    left_mean = jnp.concatenate([first, second], 1)

    own = exact_dot(left, left, 0)
    cross = exact_dot(first, lax.dynamic_slice_in_dim(second, core * PANEL, PANEL, 1), 0)
    gram = jnp.concatenate([own, cross], 1)
    gram = exchange(gram.reshape(blocks, half // blocks, half + PANEL), ROWS).sum(0)
    gram = gather(gram, ROWS).reshape(half, half + PANEL)
    inverse = inverse_factor(*in_order(gram, partner(gram), core))

    wide = columns // 2
    pair = lax.dynamic_slice_in_dim(mine, core * wide, wide, 1).astype(
        f32
    ) + lax.dynamic_slice_in_dim(theirs, core * wide, wide, 1).astype(f32)
    pair = jnp.moveaxis(pair.astype(bf16).reshape(rows, depth, wide // depth), 1, 0)
    pair, _ = lax.optimization_barrier((pair, left))
    pair = exchange(pair, "z")
    mean = pair.astype(f32).sum(0) / groups
    crossed = exact_dot(mean, left_mean, 0)
    crossed = exchange(crossed.reshape(blocks, -1, rank), ROWS).sum(0)
    crossed = gather(crossed, "z").reshape(-1, rank)

    part = lax.dot_general(
        crossed, inverse, (((1,), (1,)), ((), ())), precision=HI, preferred_element_type=f32
    )
    part = gather(part.astype(bf16), ROWS)
    left_half = lax.dot_general(
        left_mean, inverse, (((1,), (1,)), ((), ())), precision=HI, preferred_element_type=f32
    ).astype(bf16)
    right_mean = jnp.stack(in_order(part, partner(part), core), 0)
    right_mean = right_mean.reshape(2, blocks, depth, -1, rank)
    right_mean = jnp.moveaxis(right_mean, 2, 1).reshape(columns, rank)

    squares = jnp.sum(jnp.square(right_mean.astype(f32)), axis=0)
    norm = jnp.sqrt(squares / columns + tiny)
    short = columns // blocks
    new_right = lax.dynamic_slice_in_dim(right_mean, me * short, short, 0).astype(f32) / norm
    scaled = (right_mean.astype(f32) / norm).astype(bf16)
    turn = (((1,), (1,)), ((), ()))
    feedback = lax.dot_general(left_half, right_mean, turn, preferred_element_type=f32)
    update = lax.dot_general(left_half, scaled, turn, preferred_element_type=f32)
    new_momentum = combined - momentum_keep * feedback
    new_weights = (weights.astype(f32) - learn_rate * jnp.sqrt(M / N) * update).astype(bf16)
    return (new_weights, new_momentum[None], new_right)


def solution(mesh):
    split = Mesh(mesh.devices.reshape(mesh.shape["rep"] // 2, 2, 4, 4), ("z", "c", "y", "x"))
    in_specs = (P(ROWS, None), P(REP, ROWS, None), P(REP, ROWS, None), P(ROWS, None))
    out_specs = (P(ROWS, None), P(REP, ROWS, None), P(ROWS, None))
    return jax.shard_map(
        per_device, mesh=split, in_specs=in_specs, out_specs=out_specs, check_vma=False
    )
```

```python
import jax
import jax.numpy as jnp
from jax import lax
from jax.experimental import pallas as pl
from jax.experimental.pallas import tpu as pltpu
from jax.sharding import Mesh
from jax.sharding import PartitionSpec as P

M = 7168
N = 2048
ROWS = ("y", "x")
REP = ("z", "c")
SWAP = [(0, 1), (1, 0)]
PANEL = 128
HI = lax.Precision.HIGHEST
THREE = lax.Precision.HIGH
f32 = jnp.float32
bf16 = jnp.bfloat16

momentum_keep = 0.05
learn_rate = 0.5
tiny = 1e-06


def eliminate(block):
    sub = lax.broadcasted_iota(jnp.int32, (8, PANEL), 0)
    lane = lax.broadcasted_iota(jnp.int32, (8, PANEL), 1)
    tiles = PANEL // 8
    rows = [block[8 * r : 8 * r + 8, :] for r in range(tiles)]
    pivots = []
    for m in range(tiles):
        here = (lane >= 8 * m) & (lane < 8 * m + 8)
        at = [8 * m + k for k in range(8)]
        cols = [jnp.broadcast_to(rows[m][:, i : i + 1], (8, PANEL)) for i in at]
        low = jnp.where(here, jnp.where(lane - 8 * m == sub, 1.0, 0.0), rows[m])
        full = low
        pivot = jnp.zeros((8, PANEL), f32)
        for k in range(8):
            col = cols[k]
            head = jnp.broadcast_to(col[k : k + 1, :], (8, PANEL))
            inv = 1.0 / head
            pivot = jnp.where(sub == k, head, pivot)

            def step(value):
                row = jnp.broadcast_to(value[k : k + 1, :], (8, PANEL)) * inv
                return jnp.where(sub == k, row, value - col * row)

            if k < 7:
                row = jnp.broadcast_to(low[k : k + 1, :], (8, PANEL)) * inv
                low = jnp.where(sub > k, low - col * row, low)
            cols = [step(other) if n > k else other for n, other in enumerate(cols)]
            full = step(full)
        solved = [jnp.broadcast_to(full[k : k + 1, :], (8, PANEL)) for k in range(8)]
        for r in range(m + 1, tiles):
            parts = [
                jnp.broadcast_to(rows[r][:, i : i + 1], (8, PANEL)) * solved[k]
                for k, i in enumerate(at)
            ]
            while len(parts) > 1:
                parts = [parts[n] + parts[n + 1] for n in range(0, len(parts), 2)]
            rows[r] = jnp.where(here, 0.0, rows[r]) - parts[0]
        rows[m] = low
        pivots.append(pivot)
    return jnp.concatenate(rows, 0), jnp.concatenate(pivots, 0)


def exact_dot(a, b, dim=1, other=0, precision=HI):
    dims = (((dim,), (other,)), ((), ()))
    return lax.dot_general(a, b, dims, precision=precision, preferred_element_type=f32)


def panels(work_ref, out_ref, which):
    size = out_ref.shape[0]
    row = lax.broadcasted_iota(jnp.int32, (PANEL, PANEL), 0)
    lane = lax.broadcasted_iota(jnp.int32, (PANEL, PANEL), 1)
    for p in which:
        a, b = p * PANEL, (p + 1) * PANEL
        packed, pivot = eliminate(work_ref[a:b, a:b])
        lower = jnp.where(lane <= row, packed, 0.0)
        scale = lax.rsqrt(pivot)
        out_ref[a:b, a:b] = lower * scale
        if p > 0:
            left = exact_dot(lower, work_ref[a:b, :a])
            out_ref[a:b, :a] = left * jnp.concatenate([scale] * p, 1)
        if b < size:
            right = exact_dot(lower, work_ref[a:b, b:])
            out_ref[a:b, b:] = jnp.zeros((PANEL, size - b), f32)
            down = right * jnp.concatenate([1.0 / pivot] * ((size - b) // PANEL), 1)
            work_ref[b:, b:] = work_ref[b:, b:] - exact_dot(down, right, 0)
            work_ref[b:, a:b] = -exact_dot(down, lower, 0)
            if p > 0:
                work_ref[b:, :a] = work_ref[b:, :a] - exact_dot(down, left, 0)


def upper_kernel(first_ref, second_ref, out_ref):
    size = out_ref.shape[0]
    half = size // 2
    out_ref[:half, :half] = first_ref[:, :half]
    out_ref[:half, half : half + PANEL] = first_ref[:, half:]
    out_ref[:half, half + PANEL :] = second_ref[:, half:]
    out_ref[half:, half:] = second_ref[:, :half]
    panels(out_ref, out_ref, range(size // PANEL // 2))


def lower_kernel(in_ref, out_ref):
    size = out_ref.shape[0]
    out_ref[...] = in_ref[...]
    panels(out_ref, out_ref, range(size // PANEL // 2, size // PANEL))


def half_factor(kernel, size, *operands):
    space = pl.BlockSpec(memory_space=pltpu.VMEM)
    return pl.pallas_call(
        kernel,
        out_shape=jax.ShapeDtypeStruct((size, size), f32),
        in_specs=[space] * len(operands),
        out_specs=space,
        cost_estimate=pl.CostEstimate(
            flops=6_000_000_000, bytes_accessed=2_000_000, transcendentals=1000
        ),
    )(*operands)


def exchange(value, axes):
    return lax.all_to_all(value, axes, 0, 0, tiled=True)


def gather(value, axes):
    size = lax.axis_size(axes)
    return exchange(jnp.broadcast_to(value[None], (size, *value.shape)), axes)


def partner(value):
    return lax.ppermute(value, "c", SWAP)


def in_order(mine, theirs, core):
    first = jnp.where(core == 0, mine, theirs)
    second = jnp.where(core == 0, theirs, mine)
    return first, second


def per_device(weights, momentum, gradient, right_factor):
    core = lax.axis_index("c")
    depth = lax.axis_size("z")
    blocks = lax.axis_size(ROWS)
    groups = depth * lax.axis_size("c")
    me = lax.axis_index(ROWS)
    rank = right_factor.shape[1]
    half = rank // 2
    rows, columns = momentum.shape[1:]

    right_half = lax.dynamic_slice_in_dim(right_factor, core * half, half, 1).astype(bf16)
    right_half = gather(right_half, ROWS).reshape(columns, half)

    combined = momentum[0] + gradient[0].astype(f32)
    mine = combined.astype(bf16)
    theirs = partner(mine)

    left = jnp.dot(mine, right_half, preferred_element_type=f32) + jnp.dot(
        theirs, right_half, preferred_element_type=f32
    )
    left = exchange(left.astype(bf16).reshape(depth, rows // depth, half), "z")
    left = left.astype(f32).sum(0) / groups
    left = gather(left, "z").reshape(rows, half)
    first, second = in_order(left, partner(left), core)
    left_mean = jnp.concatenate([first, second], 1)

    own = exact_dot(left, left, 0)
    cross = exact_dot(first, lax.dynamic_slice_in_dim(second, core * PANEL, PANEL, 1), 0)
    gram = jnp.concatenate([own, cross], 1)
    gram = exchange(gram.reshape(blocks, half // blocks, half + PANEL), ROWS)
    gram = gram.sum(0)
    gram = gather(gram, ROWS).reshape(half, half + PANEL)
    mirrored = partner(gram)
    mirrored = in_order(gram, mirrored, core)
    inverse = half_factor(upper_kernel, rank, *mirrored)
    inverse = half_factor(lower_kernel, rank, inverse)

    wide = columns // 2
    place = lax.axis_index("z")
    width = wide // depth
    terms = []
    for shift in range(depth):
        at = core * wide + lax.rem(place + shift, depth) * width
        term = lax.dynamic_slice_in_dim(mine, at, width, 1).astype(f32)
        term = (term + lax.dynamic_slice_in_dim(theirs, at, width, 1).astype(f32)).astype(bf16)
        if shift > 0:
            term, _ = lax.optimization_barrier((term, left))
            term = lax.ppermute(term, "z", [(n, (n + shift) % depth) for n in range(depth)])
        terms.append(term)
    terms, _ = lax.optimization_barrier((terms, gram))
    mean = sum(term.astype(f32) for term in terms) / groups
    crossed = exact_dot(mean, left_mean, 0, 0, THREE)
    crossed = exchange(crossed.reshape(blocks, -1, rank), ROWS)
    crossed = crossed.sum(0)
    crossed = gather(crossed, "z").reshape(-1, rank)

    turn = (((1,), (1,)), ((), ()))
    part = exact_dot(crossed, inverse, 1, 1, THREE)
    part = gather(part.astype(bf16), ROWS)
    left_half = exact_dot(left_mean, inverse, 1, 1, THREE).astype(bf16)
    right_mean = jnp.stack(in_order(part, partner(part), core), 0)
    right_mean = right_mean.reshape(2, blocks, depth, -1, rank)
    right_mean = jnp.moveaxis(right_mean, 2, 1).reshape(columns, rank)

    squares = jnp.sum(jnp.square(right_mean.astype(f32)), axis=0)
    norm = jnp.sqrt(squares / columns + tiny)
    short = columns // blocks
    new_right = lax.dynamic_slice_in_dim(right_mean, me * short, short, 0).astype(f32) / norm
    scaled = (right_mean.astype(f32) / norm).astype(bf16)
    feedback = lax.dot_general(left_half, right_mean, turn, preferred_element_type=f32)
    update = lax.dot_general(left_half, scaled, turn, preferred_element_type=f32)
    new_momentum = combined - momentum_keep * feedback
    new_weights = (weights.astype(f32) - learn_rate * jnp.sqrt(M / N) * update).astype(bf16)
    return (new_weights, new_momentum[None], new_right)


def solution(mesh):
    split = Mesh(mesh.devices.reshape(mesh.shape["rep"] // 2, 2, 4, 4), ("z", "c", "y", "x"))
    in_specs = (P(ROWS, None), P(REP, ROWS, None), P(REP, ROWS, None), P(ROWS, None))
    out_specs = (P(ROWS, None), P(REP, ROWS, None), P(ROWS, None))

    return jax.shard_map(
        per_device, mesh=split, in_specs=in_specs, out_specs=out_specs, check_vma=False
    )
```

```python
import jax
import jax.numpy as jnp
from jax import lax
from jax.experimental import pallas as pl
from jax.experimental.pallas import tpu as pltpu
from jax.sharding import Mesh
from jax.sharding import PartitionSpec as P

M = 7168
N = 2048
ROWS = ("y", "x")
REP = ("z", "c")
SWAP = [(0, 1), (1, 0)]
PANEL = 128
HI = lax.Precision.HIGHEST
THREE = lax.Precision.HIGH
f32 = jnp.float32
bf16 = jnp.bfloat16

momentum_keep = 0.05
learn_rate = 0.5
tiny = 1e-06


def eliminate(block):
    sub = lax.broadcasted_iota(jnp.int32, (8, PANEL), 0)
    lane = lax.broadcasted_iota(jnp.int32, (8, PANEL), 1)
    tiles = PANEL // 8
    rows = [block[8 * r : 8 * r + 8, :] for r in range(tiles)]
    pivots = []
    for m in range(tiles):
        here = (lane >= 8 * m) & (lane < 8 * m + 8)
        at = [8 * m + k for k in range(8)]
        cols = [jnp.broadcast_to(rows[m][:, i : i + 1], (8, PANEL)) for i in at]
        low = jnp.where(here, jnp.where(lane - 8 * m == sub, 1.0, 0.0), rows[m])
        full = low
        pivot = jnp.zeros((8, PANEL), f32)
        for k in range(8):
            col = cols[k]
            head = jnp.broadcast_to(col[k : k + 1, :], (8, PANEL))
            inv = 1.0 / head
            pivot = jnp.where(sub == k, head, pivot)

            def step(value):
                row = jnp.broadcast_to(value[k : k + 1, :], (8, PANEL)) * inv
                return jnp.where(sub == k, row, value - col * row)

            if k < 7:
                row = jnp.broadcast_to(low[k : k + 1, :], (8, PANEL)) * inv
                low = jnp.where(sub > k, low - col * row, low)
            cols = [step(other) if n > k else other for n, other in enumerate(cols)]
            full = step(full)
        solved = [jnp.broadcast_to(full[k : k + 1, :], (8, PANEL)) for k in range(8)]
        for r in range(m + 1, tiles):
            parts = [
                jnp.broadcast_to(rows[r][:, i : i + 1], (8, PANEL)) * solved[k]
                for k, i in enumerate(at)
            ]
            while len(parts) > 1:
                parts = [parts[n] + parts[n + 1] for n in range(0, len(parts), 2)]
            rows[r] = jnp.where(here, 0.0, rows[r]) - parts[0]
        rows[m] = low
        pivots.append(pivot)
    return jnp.concatenate(rows, 0), jnp.concatenate(pivots, 0)


def exact_dot(a, b, dim=1, other=0, precision=HI):
    dims = (((dim,), (other,)), ((), ()))
    return lax.dot_general(a, b, dims, precision=precision, preferred_element_type=f32)


def panels(work_ref, out_ref, which):
    size = out_ref.shape[0]
    row = lax.broadcasted_iota(jnp.int32, (PANEL, PANEL), 0)
    lane = lax.broadcasted_iota(jnp.int32, (PANEL, PANEL), 1)
    for p in which:
        a, b = p * PANEL, (p + 1) * PANEL
        packed, pivot = eliminate(work_ref[a:b, a:b])
        lower = jnp.where(lane <= row, packed, 0.0)
        scale = lax.rsqrt(pivot)
        out_ref[a:b, a:b] = lower * scale
        if p > 0:
            left = exact_dot(lower, work_ref[a:b, :a])
            out_ref[a:b, :a] = left * jnp.concatenate([scale] * p, 1)
        if b < size:
            right = exact_dot(lower, work_ref[a:b, b:])
            out_ref[a:b, b:] = jnp.zeros((PANEL, size - b), f32)
            down = right * jnp.concatenate([1.0 / pivot] * ((size - b) // PANEL), 1)
            work_ref[b:, b:] = work_ref[b:, b:] - exact_dot(down, right, 0)
            work_ref[b:, a:b] = -exact_dot(down, lower, 0)
            if p > 0:
                work_ref[b:, :a] = work_ref[b:, :a] - exact_dot(down, left, 0)


def upper_kernel(first_ref, second_ref, out_ref):
    size = out_ref.shape[0]
    half = size // 2
    out_ref[:half, :half] = first_ref[:, :half]
    out_ref[:half, half : half + PANEL] = first_ref[:, half:]
    out_ref[:half, half + PANEL :] = second_ref[:, half:]
    out_ref[half:, half:] = second_ref[:, :half]
    panels(out_ref, out_ref, range(size // PANEL // 2))


def lower_kernel(in_ref, out_ref):
    size = out_ref.shape[0]
    out_ref[...] = in_ref[...]
    panels(out_ref, out_ref, range(size // PANEL // 2, size // PANEL))


def half_factor(kernel, size, *operands):
    space = pl.BlockSpec(memory_space=pltpu.VMEM)
    return pl.pallas_call(
        kernel,
        out_shape=jax.ShapeDtypeStruct((size, size), f32),
        in_specs=[space] * len(operands),
        out_specs=space,
        cost_estimate=pl.CostEstimate(
            flops=6_000_000_000, bytes_accessed=2_000_000, transcendentals=1000
        ),
    )(*operands)


def tile_rows(ref, pair):
    parts = []
    for z in (0, 1):
        part = ref[:, 2 * pair + z].astype(f32)
        parts.append(part.reshape(-1, part.shape[-1]))
    return jnp.concatenate(parts, 0)


def outer(left, right):
    return lax.dot_general(left, right, (((1,), (1,)), ((), ())), preferred_element_type=f32)


def own_kernel(where_ref, part_ref, left_ref, momentum_ref, gradient_ref, out_ref):
    right = tile_rows(part_ref, pl.program_id(0)).astype(bf16)
    feedback = outer(left_ref[...], right)
    combined = momentum_ref[...] + gradient_ref[...].astype(f32)
    out_ref[...] = combined - momentum_keep * feedback


def rest_kernel(
    where_ref,
    mine_ref,
    theirs_ref,
    left_ref,
    momentum_ref,
    gradient_ref,
    weights_ref,
    done_ref,
    momentum_out,
    weights_out,
    right_out,
    norm_ref,
    right_ref,
):
    step = pl.program_id(0)
    steps = pl.num_programs(0) // 2
    depth = mine_ref.shape[1]

    @pl.when(step == 0)
    def _():
        squares = jnp.zeros(norm_ref.shape, f32)
        count = 0
        for ref in (mine_ref, theirs_ref):
            for z in range(depth):
                squares = squares + jnp.sum(jnp.square(ref[:, z].astype(f32)), axis=0)
            count += ref.shape[0] * depth * ref.shape[2]
        total = jnp.sum(squares, axis=0, keepdims=True)
        norm_ref[...] = jnp.broadcast_to(1.0 / jnp.sqrt(total / count + tiny), norm_ref.shape)
        for ref, owner in ((mine_ref, where_ref[0]), (theirs_ref, 1 - where_ref[0])):

            @pl.when(where_ref[1] // depth == owner)
            def _():
                value = ref[:, lax.rem(where_ref[1], depth)].astype(f32) * norm_ref[...][None]
                right_out[...] = value.reshape(right_out.shape)

    @pl.when(step < steps)
    def _():
        right = tile_rows(theirs_ref, step)
        right_ref[...] = right
        feedback = outer(left_ref[...], right.astype(bf16))
        combined = momentum_ref[...] + gradient_ref[...].astype(f32)
        momentum_out[...] = combined - momentum_keep * feedback

    @pl.when(step >= steps)
    def _():
        right_ref[...] = tile_rows(mine_ref, step - steps)

    scaled = (right_ref[...] * norm_ref[0:1, :]).astype(bf16)
    update = outer(left_ref[...], scaled)
    value = weights_ref[...].astype(f32) - (learn_rate * (M / N) ** 0.5) * update
    weights_out[...] = value.astype(bf16)


def final_specs(part, left, half, tile):
    whole = pl.BlockSpec(part.shape, lambda j, w: (0, 0, 0, 0))
    factor = pl.BlockSpec(left.shape, lambda j, w: (0, 0))
    rows = left.shape[0]
    own = pl.BlockSpec((rows, tile), lambda j, w: (0, w[0] * half + j))
    rest = pl.BlockSpec((rows, tile), lambda j, w: (0, (1 - w[0]) * half + jnp.minimum(j, half - 1)))
    both = pl.BlockSpec(
        (rows, tile), lambda j, w: (0, jnp.where(j < half, (1 - w[0]) * half + j, w[0] * half + j - half))
    )
    return whole, factor, own, rest, both


def finish_own(where, part, left, momentum, gradient):
    tile = 256
    half = momentum.shape[1] // tile // 2
    whole, factor, own, _, _ = final_specs(part, left, half, tile)
    return pl.pallas_call(
        own_kernel,
        out_shape=jax.ShapeDtypeStruct(momentum.shape, f32),
        grid_spec=pltpu.PrefetchScalarGridSpec(
            num_scalar_prefetch=1, grid=(half,), in_specs=[whole, factor, own, own], out_specs=own
        ),
        cost_estimate=pl.CostEstimate(
            flops=1_000_000_000, bytes_accessed=6_000_000, transcendentals=0
        ),
        name="finish_own",
    )(where, part, left, momentum, gradient)


def finish_rest(where, mine, theirs, left, momentum, gradient, weights, done):
    tile = 256
    half = momentum.shape[1] // tile // 2
    whole, factor, _, rest, both = final_specs(mine, left, half, tile)
    rank = left.shape[1]
    short = mine.shape[0] * mine.shape[2]
    return pl.pallas_call(
        rest_kernel,
        out_shape=[
            jax.ShapeDtypeStruct(momentum.shape, f32),
            jax.ShapeDtypeStruct(weights.shape, bf16),
            jax.ShapeDtypeStruct((short, rank), f32),
        ],
        grid_spec=pltpu.PrefetchScalarGridSpec(
            num_scalar_prefetch=1,
            grid=(2 * half,),
            in_specs=[whole, whole, factor, rest, rest, both, pl.BlockSpec(memory_space=pl.ANY)],
            out_specs=[rest, both, pl.BlockSpec((short, rank), lambda j, w: (0, 0))],
            scratch_shapes=[pltpu.VMEM((8, rank), f32), pltpu.VMEM((tile, rank), f32)],
        ),
        input_output_aliases={7: 0},
        cost_estimate=pl.CostEstimate(
            flops=2_000_000_000, bytes_accessed=12_000_000, transcendentals=1000
        ),
        name="finish_rest",
    )(where, mine, theirs, left, momentum, gradient, weights, done)


def exchange(value, axes):
    return lax.all_to_all(value, axes, 0, 0, tiled=True)


def gather(value, axes):
    size = lax.axis_size(axes)
    return exchange(jnp.broadcast_to(value[None], (size, *value.shape)), axes)


def partner(value):
    return lax.ppermute(value, "c", SWAP)


def in_order(mine, theirs, core):
    first = jnp.where(core == 0, mine, theirs)
    second = jnp.where(core == 0, theirs, mine)
    return first, second


def per_device(weights, momentum, gradient, right_factor):
    core = lax.axis_index("c")
    depth = lax.axis_size("z")
    blocks = lax.axis_size(ROWS)
    groups = depth * lax.axis_size("c")
    me = lax.axis_index(ROWS)
    rank = right_factor.shape[1]
    half = rank // 2
    rows, columns = momentum.shape[1:]

    right_half = lax.dynamic_slice_in_dim(right_factor, core * half, half, 1).astype(bf16)
    right_half = gather(right_half, ROWS).reshape(columns, half)

    combined = momentum[0] + gradient[0].astype(f32)
    mine = combined.astype(bf16)
    theirs = partner(mine)

    pair = (mine.astype(f32) + theirs.astype(f32)).astype(bf16)
    left = jnp.dot(pair, right_half, preferred_element_type=f32)
    left = exchange(left.astype(bf16).reshape(depth, rows // depth, half), "z")
    left = left.astype(f32).sum(0) / groups
    left = gather(left, "z").reshape(rows, half)
    first, second = in_order(left, partner(left), core)
    left_mean = jnp.concatenate([first, second], 1)

    own = exact_dot(left, left, 0)
    cross = exact_dot(first, lax.dynamic_slice_in_dim(second, core * PANEL, PANEL, 1), 0)
    gram = jnp.concatenate([own, cross], 1)
    gram = exchange(gram.reshape(blocks, half // blocks, half + PANEL), ROWS)
    gram = gram.sum(0)
    gram = gather(gram, ROWS).reshape(half, half + PANEL)
    mirrored = partner(gram)
    mirrored = in_order(gram, mirrored, core)
    inverse = half_factor(upper_kernel, rank, *mirrored)
    inverse = half_factor(lower_kernel, rank, inverse)

    wide = columns // 2
    place = lax.axis_index("z")
    width = wide // depth
    terms = []
    for shift in range(depth):
        at = core * wide + lax.rem(place + shift, depth) * width
        term = lax.dynamic_slice_in_dim(pair, at, width, 1)
        if shift > 0:
            term, _ = lax.optimization_barrier((term, left))
            term = lax.ppermute(term, "z", [(n, (n + shift) % depth) for n in range(depth)])
        terms.append(term)
    terms, _ = lax.optimization_barrier((terms, gram))
    mean = sum(term.astype(f32) for term in terms) / groups
    crossed = exact_dot(mean, left_mean, 0, 0, THREE)
    crossed = exchange(crossed.reshape(blocks, -1, rank), ROWS)
    crossed = crossed.sum(0)
    crossed = gather(crossed, "z").reshape(-1, rank)

    part = exact_dot(crossed, inverse, 1, 1, THREE)
    part = gather(part.astype(bf16), ROWS)
    left_half = exact_dot(left_mean, inverse, 1, 1, THREE).astype(bf16)
    part = part.reshape(blocks, depth, -1, rank)
    other = partner(part)
    where = jnp.where(jnp.arange(2) == 0, core, me).astype(jnp.int32)
    moved = finish_own(where, part, left_half, momentum[0], gradient[0])
    moved, new_weights, new_right = finish_rest(
        where, part, other, left_half, momentum[0], gradient[0], weights, moved
    )
    return (new_weights, moved[None], new_right)


def solution(mesh):
    split = Mesh(mesh.devices.reshape(mesh.shape["rep"] // 2, 2, 4, 4), ("z", "c", "y", "x"))
    in_specs = (P(ROWS, None), P(REP, ROWS, None), P(REP, ROWS, None), P(ROWS, None))
    out_specs = (P(ROWS, None), P(REP, ROWS, None), P(ROWS, None))

    return jax.shard_map(
        per_device, mesh=split, in_specs=in_specs, out_specs=out_specs, check_vma=False
    )
```

```python
import jax
import jax.numpy as jnp
from jax import lax
from jax.experimental import pallas as pl
from jax.experimental.pallas import tpu as pltpu
from jax.sharding import Mesh
from jax.sharding import PartitionSpec as P

M = 7168
N = 2048
ROWS = ("y", "x")
REP = ("z", "c")
SWAP = [(0, 1), (1, 0)]
PANEL = 128
HI = lax.Precision.HIGHEST
THREE = lax.Precision.HIGH
f32 = jnp.float32
bf16 = jnp.bfloat16

momentum_keep = 0.05
learn_rate = 0.5
tiny = 1e-06


def eliminate(block):
    sub = lax.broadcasted_iota(jnp.int32, (8, PANEL), 0)
    lane = lax.broadcasted_iota(jnp.int32, (8, PANEL), 1)
    tiles = PANEL // 8
    rows = [block[8 * r : 8 * r + 8, :] for r in range(tiles)]
    pivots = []
    for m in range(tiles):
        here = (lane >= 8 * m) & (lane < 8 * m + 8)
        at = [8 * m + k for k in range(8)]
        cols = [jnp.broadcast_to(rows[m][:, i : i + 1], (8, PANEL)) for i in at]
        low = jnp.where(here, jnp.where(lane - 8 * m == sub, 1.0, 0.0), rows[m])
        full = low
        pivot = jnp.zeros((8, PANEL), f32)
        for k in range(8):
            col = cols[k]
            head = jnp.broadcast_to(col[k : k + 1, :], (8, PANEL))
            inv = 1.0 / head
            pivot = jnp.where(sub == k, head, pivot)

            def step(value):
                row = jnp.broadcast_to(value[k : k + 1, :], (8, PANEL)) * inv
                return jnp.where(sub == k, row, value - col * row)

            if k < 7:
                row = jnp.broadcast_to(low[k : k + 1, :], (8, PANEL)) * inv
                low = jnp.where(sub > k, low - col * row, low)
            cols = [step(other) if n > k else other for n, other in enumerate(cols)]
            full = step(full)
        solved = [jnp.broadcast_to(full[k : k + 1, :], (8, PANEL)) for k in range(8)]
        for r in range(m + 1, tiles):
            parts = [
                jnp.broadcast_to(rows[r][:, i : i + 1], (8, PANEL)) * solved[k]
                for k, i in enumerate(at)
            ]
            while len(parts) > 1:
                parts = [parts[n] + parts[n + 1] for n in range(0, len(parts), 2)]
            rows[r] = jnp.where(here, 0.0, rows[r]) - parts[0]
        rows[m] = low
        pivots.append(pivot)
    return jnp.concatenate(rows, 0), jnp.concatenate(pivots, 0)


def exact_dot(a, b, dim=1, other=0, precision=HI):
    dims = (((dim,), (other,)), ((), ()))
    return lax.dot_general(a, b, dims, precision=precision, preferred_element_type=f32)


def panels(work_ref, out_ref, which):
    size = out_ref.shape[0]
    row = lax.broadcasted_iota(jnp.int32, (PANEL, PANEL), 0)
    lane = lax.broadcasted_iota(jnp.int32, (PANEL, PANEL), 1)
    for p in which:
        a, b = p * PANEL, (p + 1) * PANEL
        packed, pivot = eliminate(work_ref[a:b, a:b])
        lower = jnp.where(lane <= row, packed, 0.0)
        scale = lax.rsqrt(pivot)
        out_ref[a:b, a:b] = lower * scale
        if p > 0:
            left = exact_dot(lower, work_ref[a:b, :a])
            out_ref[a:b, :a] = left * jnp.concatenate([scale] * p, 1)
        if b < size:
            right = exact_dot(lower, work_ref[a:b, b:])
            out_ref[a:b, b:] = jnp.zeros((PANEL, size - b), f32)
            down = right * jnp.concatenate([1.0 / pivot] * ((size - b) // PANEL), 1)
            work_ref[b:, b:] = work_ref[b:, b:] - exact_dot(down, right, 0)
            work_ref[b:, a:b] = -exact_dot(down, lower, 0)
            if p > 0:
                work_ref[b:, :a] = work_ref[b:, :a] - exact_dot(down, left, 0)


def upper_kernel(first_ref, second_ref, out_ref):
    size = out_ref.shape[0]
    half = size // 2
    out_ref[:half, :half] = first_ref[:, :half]
    out_ref[:half, half : half + PANEL] = first_ref[:, half:]
    out_ref[:half, half + PANEL :] = second_ref[:, half:]
    out_ref[half:, half:] = second_ref[:, :half]
    panels(out_ref, out_ref, range(size // PANEL // 2))


def lower_kernel(in_ref, out_ref):
    size = out_ref.shape[0]
    out_ref[...] = in_ref[...]
    panels(out_ref, out_ref, range(size // PANEL // 2, size // PANEL))


def half_factor(kernel, size, *operands):
    space = pl.BlockSpec(memory_space=pltpu.VMEM)
    return pl.pallas_call(
        kernel,
        out_shape=jax.ShapeDtypeStruct((size, size), f32),
        in_specs=[space] * len(operands),
        out_specs=space,
        cost_estimate=pl.CostEstimate(
            flops=6_000_000_000, bytes_accessed=2_000_000, transcendentals=1000
        ),
        compiler_params=pltpu.CompilerParams(vmem_limit_bytes=8 << 20),
    )(*operands)


def exchange(value, axes):
    return lax.all_to_all(value, axes, 0, 0, tiled=True)


def gather(value, axes):
    size = lax.axis_size(axes)
    return exchange(jnp.broadcast_to(value[None], (size, *value.shape)), axes)


def partner(value):
    return lax.ppermute(value, "c", SWAP)


def in_order(mine, theirs, core):
    first = jnp.where(core == 0, mine, theirs)
    second = jnp.where(core == 0, theirs, mine)
    return first, second


def per_device(weights, momentum, gradient, right_factor):
    core = lax.axis_index("c")
    depth = lax.axis_size("z")
    blocks = lax.axis_size(ROWS)
    groups = depth * lax.axis_size("c")
    me = lax.axis_index(ROWS)
    rank = right_factor.shape[1]
    half = rank // 2
    rows, columns = momentum.shape[1:]

    right_half = lax.dynamic_slice_in_dim(right_factor, core * half, half, 1).astype(bf16)
    right_half = gather(right_half, ROWS).reshape(columns, half)

    combined = momentum[0] + gradient[0].astype(f32)
    mine = combined.astype(bf16)
    theirs = partner(mine)

    pair = (mine.astype(f32) + theirs.astype(f32)).astype(bf16)
    left = jnp.dot(pair, right_half, preferred_element_type=f32)
    left = exchange(left.astype(bf16).reshape(depth, rows // depth, half), "z")
    left = left.astype(f32).sum(0) / groups
    left = gather(left, "z").reshape(rows, half)
    first, second = in_order(left, partner(left), core)
    left_mean = jnp.concatenate([first, second], 1)

    own = exact_dot(left, left, 0)
    cross = exact_dot(first, lax.dynamic_slice_in_dim(second, core * PANEL, PANEL, 1), 0)
    gram = jnp.concatenate([own, cross], 1)
    gram = exchange(gram.reshape(blocks, half // blocks, half + PANEL), ROWS)
    gram = gram.sum(0)
    gram = gather(gram, ROWS).reshape(half, half + PANEL)
    mirrored = partner(gram)
    mirrored = in_order(gram, mirrored, core)
    inverse = half_factor(upper_kernel, rank, *mirrored)
    inverse = half_factor(lower_kernel, rank, inverse)

    wide = columns // 2
    place = lax.axis_index("z")
    width = wide // depth
    terms = []
    for shift in range(depth):
        at = core * wide + lax.rem(place + shift, depth) * width
        term = lax.dynamic_slice_in_dim(pair, at, width, 1)
        if shift > 0:
            term, _ = lax.optimization_barrier((term, left))
            term = lax.ppermute(term, "z", [(n, (n + shift) % depth) for n in range(depth)])
        terms.append(term)
    terms, _ = lax.optimization_barrier((terms, gram))
    mean = sum(term.astype(f32) for term in terms) / groups
    crossed = exact_dot(mean, left_mean, 0, 0, THREE)
    crossed = exchange(crossed.reshape(blocks, -1, rank), ROWS)
    crossed = crossed.sum(0)
    crossed = gather(crossed, "z").reshape(-1, rank)

    turn = (((1,), (1,)), ((), ()))
    part = exact_dot(crossed, inverse, 1, 1, THREE)
    part = gather(part.astype(bf16), ROWS)
    left_half = exact_dot(left_mean, inverse, 1, 1, THREE).astype(bf16)
    other = partner(part)
    right_mean = jnp.stack(in_order(part, other, core), 0)
    right_mean = right_mean.reshape(2, blocks, depth, -1, rank)
    right_mean = jnp.moveaxis(right_mean, 2, 1).reshape(columns, rank)

    squares = jnp.sum(jnp.square(right_mean.astype(f32)), axis=0)
    norm = jnp.sqrt(squares / columns + tiny)
    short = columns // blocks
    new_right = lax.dynamic_slice_in_dim(right_mean, me * short, short, 0).astype(f32) / norm
    scaled = (right_mean.astype(f32) / norm).astype(bf16)
    turn = (((1,), (1,)), ((), ()))
    feedback = lax.dot_general(left_half, right_mean, turn, preferred_element_type=f32)
    update = lax.dot_general(left_half, scaled, turn, preferred_element_type=f32)
    new_momentum = mine.astype(f32) - momentum_keep * feedback
    new_weights = (weights.astype(f32) - learn_rate * jnp.sqrt(M / N) * update).astype(bf16)
    return (new_weights, new_momentum[None], new_right)


def solution(mesh):
    split = Mesh(mesh.devices.reshape(mesh.shape["rep"] // 2, 2, 4, 4), ("z", "c", "y", "x"))
    in_specs = (P(ROWS, None), P(REP, ROWS, None), P(REP, ROWS, None), P(ROWS, None))
    out_specs = (P(ROWS, None), P(REP, ROWS, None), P(ROWS, None))

    return jax.shard_map(
        per_device, mesh=split, in_specs=in_specs, out_specs=out_specs, check_vma=False
    )
```
